32 devices in a mesh: cols: 8 (over y, x, core), rows: 4 (over z).
Axes of the slice: x: 2, y: 2, z: 4, core: 2. Of those that a mesh axis runs over, the one named last changes fastest.
Arguments:
- panel: bfloat16 [8, 24, 1024, 128], P('rows', 'cols'), may hold values from -0.1875 to 0.1875
- row_k: bfloat16 [24, 1024, 128], P('cols', 'rows'), as said below
- mask: int32 [8, 24], P('rows', 'cols'), may hold values 0 or 1
- a_low: bfloat16 [8, 1024, 128], P('rows'), may hold values from -0.375 to 0.375
- a_diag: float32 [1024, 1024], P('rows'), as said below
- sketch: bfloat16 [1024, 64], replicated, may hold values from -6 to 6
Outputs:
- panel_out: float32 [8, 1024, 128], P('rows')
- diag_factor: float32 [1024, 1024], P('rows')
The draws below stay inside these ranges and needn't reach their ends.
Inputs may be any that keep to these rules, and one draw needn't show every extreme that they name: row_k entries are normal with deviation 1024 ** -0.5, cut at six deviations. a_diag - update is symmetric, with every eigenvalue 2 or more.
All inputs are finite; a program needn't handle non-finite values. No bound on the sum of `mask` on one device may be relied on, other than what follows from the above.
Results may differ from the reference program's by a relative error of at most 0.02.
Values may be sent and summed in bfloat16 or wider, within the bound.
No kernel may reach another device: no remote copies, remote signals or barrier semaphores. Data moves between devices by JAX's collectives and lax.ppermute only.
A program may use at most 128 MiB of HBM per device.

```python
import jax
import jax.numpy as jnp
from jax import lax

B = 1024
R = 64
P_SIZE = 64
TR_TOT = 8
JTOT = 24


def row_values(key):
    base = jax.random.fold_in(key, 101)
    values = jax.random.normal(base, (JTOT, B, 2 * R), jnp.float32)
    values = jnp.clip(values, -6.0, 6.0) * jnp.float32(B) ** (-0.5)
    return values.astype(jnp.bfloat16)


def draw_row_k(key, part):
    return row_values(key)


def draw_a_diag(key, part):
    factors = row_values(key).astype(jnp.float32)
    k_left = factors[..., :R]
    k_right = factors[..., R:]
    high = lax.Precision.HIGHEST
    diag_core = jnp.einsum('jbr,jbs->jrs', k_right, k_right, precision=high).astype(jnp.bfloat16).astype(jnp.float32)
    k_mixed = jnp.einsum('jbr,jrs->jbs', k_left, diag_core, precision=high).astype(jnp.bfloat16).astype(jnp.float32)
    update = jnp.einsum('jbs,jcs->bc', k_mixed, k_left, precision=high)
    mixing = jnp.clip(jax.random.normal(jax.random.fold_in(key, 202), (B, B), jnp.float32), -6.0, 6.0)
    covar = jnp.einsum('bk,ck->bc', mixing, mixing, precision=high) / jnp.float32(B)
    covar = 0.5 * (covar + covar.T)
    return 2.0 * jnp.eye(B, dtype=jnp.float32) + covar + update


def touch_ends(drawn, key, least, high):
    index_at = [jax.random.randint(jax.random.fold_in(key, axis), (), 0, length) for axis, length in enumerate(drawn.shape)]
    longest = drawn.shape.index(max(drawn.shape))
    beside = index_at[:longest] + [(index_at[longest] + 1) % drawn.shape[longest]] + index_at[longest + 1:]
    return drawn.at[tuple(index_at)].set(least).at[tuple(beside)].set(high)


def shard_levels(stream_key, dims, cuts, least, high):
    loudness = 1.0
    for dim, shards_of in cuts:
        draws = jax.random.uniform(jax.random.fold_in(jax.random.fold_in(stream_key, 6), dim), (shards_of,), jnp.float32, least / len(cuts), high / len(cuts))
        loudness = loudness * jnp.repeat(jnp.exp(draws), dims[dim] // shards_of).reshape((-1,) + (1,) * (len(dims) - 1 - dim))
    return loudness


def noise(own_key, shape, scale, reach, cuts=(), kind=jnp.bfloat16):
    entries = jax.random.normal(own_key, shape, jnp.float32) * scale
    if len(cuts) > 0:
        entries = shard_levels(own_key, shape, cuts, -0.22, 0.18) * entries
    return jnp.clip(entries, min=-reach, max=reach).astype(kind)


def setup_inputs(seed: int = 0) -> dict:
    seeds = jax.random.split(jax.random.key(seed), 7)
    return {
        "panel": noise(seeds[0], (TR_TOT, JTOT, B, 2 * R), B ** -0.5, 0.1875, ((0, 4), (1, 8))),
        "row_k": draw_row_k(jax.random.fold_in(seeds[6], 71), 0),
        "mask": touch_ends((jax.random.randint(seeds[2], (TR_TOT, JTOT), 0, 4) < 3).astype(jnp.int32), jax.random.fold_in(seeds[2], 1), 0, 1),
        "a_low": noise(seeds[3], (TR_TOT, B, 2 * R), (4 * R) ** -0.5, 0.375, ((0, 4),)),
        "a_diag": draw_a_diag(jax.random.fold_in(seeds[6], 71), 0),
        "sketch": noise(seeds[5], (B, P_SIZE), 1.0, 6.0),
    }


def mult(form, first, second):
    return jnp.einsum(form, first.astype(jnp.float32), second.astype(jnp.float32), precision=lax.Precision.HIGHEST)

def round_half(values):
    return lax.optimization_barrier(values.astype(jnp.bfloat16)).astype(jnp.float32)

def orthonormal(field):
    gram_matrix = mult('bp,bq->pq', field, field)
    lower_factor = jnp.linalg.cholesky(gram_matrix)
    return lax.linalg.triangular_solve(lower_factor, field.T, left_side=True, lower=True).T

def reference(panel, row_k, mask, a_low, a_diag, sketch):
    k_left = row_k[..., :R].astype(jnp.float32)
    k_right = row_k[..., R:].astype(jnp.float32)
    diag_core = round_half(mult('jbr,jbs->jrs', k_right, k_right))
    k_mixed = round_half(mult('jbr,jrs->jbs', k_left, diag_core))
    update = mult('jbs,jcs->bc', k_mixed, k_left)
    factor = jnp.linalg.cholesky(a_diag - update)
    omega = sketch.astype(jnp.float32)
    probe = round_half(mult('jbr,bp->jrp', k_left, omega))

    def one_row(items):
        tiles, marks, low = items
        left_part = tiles[..., :R].astype(jnp.float32)
        right_part = tiles[..., R:].astype(jnp.float32)
        a_up = low[:, :R].astype(jnp.float32)
        a_down = low[:, R:].astype(jnp.float32)
        core = round_half(mult('jbr,jbs->jrs', right_part, k_right) * marks.astype(jnp.float32)[:, None, None])
        mixed_left = round_half(mult('jbr,jrs->jbs', left_part, core))
        first = mult('br,rp->bp', a_up, round_half(mult('br,bp->rp', a_down, omega))) - mult('jbs,jsp->bp', mixed_left, probe)
        first_b = round_half(first)
        second = mult('br,rp->bp', a_down, round_half(mult('br,bp->rp', a_up, first_b))) - mult('jbr,jrp->bp', k_left, round_half(mult('jbs,bp->jsp', mixed_left, first_b)))
        second_b = round_half(second)
        third = mult('br,rp->bp', a_up, round_half(mult('br,bp->rp', a_down, second_b))) - mult('jbs,jsp->bp', mixed_left, round_half(mult('jbr,bp->jrp', k_left, second_b)))
        basis_cols = orthonormal(third)
        basis_b = round_half(basis_cols)
        projected = mult('br,rp->bp', a_down, round_half(mult('br,bp->rp', a_up, basis_b))) - mult('jbr,jrp->bp', k_left, round_half(mult('jbs,bp->jsp', mixed_left, basis_b)))
        return (basis_cols, projected)
    bases, projections = lax.map(one_row, (panel, mask, a_low))
    stacked = jnp.transpose(projections, (1, 0, 2)).reshape(B, TR_TOT * P_SIZE)
    solved = lax.linalg.triangular_solve(factor, stacked, left_side=True, lower=True).reshape(B, TR_TOT, P_SIZE)
    panel_out = jnp.concatenate([bases, jnp.transpose(solved, (1, 0, 2))], axis=2)
    return (panel_out, factor)
```

```python
import functools

import jax
import jax.numpy as jnp
from jax import lax
from jax.experimental import pallas as pl
from jax.experimental.pallas import tpu as pltpu
from jax.sharding import PartitionSpec as P

f32 = jnp.float32
bf16 = jnp.bfloat16
WIDE = 256
HALF = 128
SMEM = pl.BlockSpec(memory_space=pltpu.SMEM)
VMEM = pl.BlockSpec(memory_space=pltpu.VMEM)


def nt(first, second, **kw):
    return lax.dot_general(
        first, second, (((1,), (1,)), ((), ())), preferred_element_type=f32, **kw
    )


def tn(first, second):
    return lax.dot_general(first, second, (((0,), (0,)), ((), ())), preferred_element_type=f32)


def nn(first, second, **kw):
    return jnp.dot(first, second, preferred_element_type=f32, **kw)


def shaped(shape, kind):
    return jax.ShapeDtypeStruct(shape, kind)


def call(body, name, outs, *args, scratch=()):
    return pl.pallas_call(
        body,
        out_shape=outs,
        in_specs=[SMEM] + [VMEM] * (len(args) - 1),
        out_specs=jax.tree.map(lambda _: VMEM, outs),
        scratch_shapes=list(scratch),
        name=name,
    )(*args)


def eliminate(block):
    size = block.shape[0]
    lane = lax.broadcasted_iota(jnp.int32, (8, size), 1)
    sub = lax.broadcasted_iota(jnp.int32, (8, size), 0)
    tiles = [block[8 * g : 8 * g + 8] for g in range(size // 8)]

    def spread(tile, j):
        return jnp.broadcast_to(tile[:, j : j + 1], (8, size))

    def lift(tile, i):
        return jnp.broadcast_to(tile[i : i + 1], (8, size))

    uppers, inverses = [], []
    for own in range(size // 8):
        base = 8 * own
        tile = tiles[own]
        cols = [spread(tile, base + j) for j in range(8)]
        s = {(i, j): lift(cols[j], i) for j in range(8) for i in range(j, 8)}
        inside = (lane >= base) & (lane < base + 8)
        u = [
            jnp.where(inside, jnp.where(lane == base + i, 1.0, 0.0), lift(tile, i))
            for i in range(8)
        ]
        inv, m = [], {}
        for k in range(8):
            inv.append(1.0 / s[k, k])
            for i in range(k + 1, 8):
                m[i, k] = s[i, k] * inv[k]
            for i in range(k + 1, 8):
                for j in range(k + 1, i + 1):
                    s[i, j] = s[i, j] - m[i, k] * s[j, k]
                u[i] = u[i] - m[i, k] * u[k]
        w = [u[i] * inv[i] for i in range(8)]
        for i in range(6, -1, -1):
            for k in range(7, i, -1):
                w[i] = w[i] - m[k, i] * w[k]
        for g in range(own + 1, size // 8):
            rest = jnp.where(inside, 0.0, tiles[g])
            for j in range(7, -1, -1):
                rest = rest - spread(tiles[g], base + j) * w[j]
            tiles[g] = rest
        low = jnp.zeros((8, size), f32)
        up = jnp.zeros((8, size), f32)
        for i in range(8):
            root = lax.rsqrt(s[i, i])
            row = u[i] * root
            low = jnp.where(sub == i, row, low)
            for j in range(i, 8):
                row = jnp.where(lane == base + j, s[j, i] * root, row)
            up = jnp.where(sub == i, row, up)
        inverses.append(jnp.where(lane <= sub + base, low, 0.0))
        uppers.append(jnp.where(lane >= sub + base, up, 0.0))
    return jnp.concatenate(uppers, 0), jnp.concatenate(inverses, 0)


def prepare_body(place, row_ref, diag_ref, low_ref, sketch_ref, *outs):
    left_ref, right_ref, piece_ref, low_t_ref, sketch_t_ref = outs
    count, slab, width = row_ref.shape
    half = width // 2
    per = max(slab // half, 1)
    core, block = place[0], place[5]
    for j in range(count):
        turned = row_ref[j].astype(f32).T.astype(bf16)
        left_ref[j * half : (j + 1) * half, :] = turned[:half]
        right_ref[j * half : (j + 1) * half, :] = turned[half:]
        gram = nt(turned[half:], turned[half:])
        top = count * half + (j // per) * half
        if j % per == 0:
            left_ref[top : top + half, :] = jnp.zeros((half, slab), bf16)
        at = (j % per) * half
        left_ref[top : top + half, at : at + half] = gram.astype(bf16)
    wide = diag_ref[:, pl.ds(pl.multiple_of(block * HALF, HALF), HALF)]
    lane = lax.broadcasted_iota(jnp.int32, wide.shape, 1)
    piece_ref[...] = jnp.where((lane >= place[6]) & (lane < place[7]), wide, 0.0).astype(bf16)
    turned = low_ref[core].astype(f32).T
    low_t_ref[...] = turned.astype(bf16)
    sketch_t_ref[...] = sketch_ref[...].astype(f32).T.astype(bf16)


def diagonal_body(count, parts, place, *refs):
    lefts, pieces = refs[:parts], refs[parts : 2 * parts]
    left_ref, own0_ref, own1_ref, away0_ref, away1_ref, total, turned = refs[2 * parts :]
    slab = lefts[0].shape[1]
    half = turned.shape[0] // count
    per = max(slab // half, 1)
    core, z, block = place[0], place[1], place[5]
    for d in range(parts):
        source = lax.rem(z - d + parts, parts)
        left_ref[:, pl.ds(pl.multiple_of(source * slab, HALF), slab)] = lefts[d][: count * half]
    for j in range(count):
        rows = slice(j * half, (j + 1) * half)
        top, at = count * half + (j // per) * half, (j % per) * half
        core_sum = sum(lefts[d][top : top + half, at : at + half].astype(f32) for d in range(parts))
        turned[rows, :] = (-nn(core_sum.astype(bf16), left_ref[rows, :])).astype(bf16)
    total[...] = tn(turned[...], left_ref[...])
    for d in range(parts):
        source = lax.rem(z - d + parts, parts)
        at = (
            pl.ds(pl.multiple_of(source * slab, slab), slab),
            pl.ds(pl.multiple_of(block * HALF, HALF), HALF),
        )
        total[at] = total[at] + pieces[d][...].astype(f32)
    order = total.shape[0]
    for out0, out1, side in ((own0_ref, own1_ref, core), (away0_ref, away1_ref, 1 - core)):
        fill = 0
        for g in range(order // WIDE):
            for b in range(g, order // WIDE):
                from_row = pl.multiple_of(b * WIDE + side * HALF, HALF)
                value = total[pl.ds(from_row, HALF), g * WIDE : (g + 1) * WIDE].astype(bf16)
                if g == 0:
                    out0[b * HALF : (b + 1) * HALF, :] = value
                else:
                    out1[fill : fill + HALF, :] = value
                    fill += HALF


def factor_body(group, at, place, own_ref, other_ref, *refs):
    earlier = refs[:group]
    slab_ref, half_ref, inverse_ref, acc, whole = refs[group:]
    core, z = place[0], place[1]
    order = whole.shape[0]
    first = group * WIDE
    count = order - first
    for b in range(count // WIDE):
        rows = slice(at + b * HALF, at + (b + 1) * HALF)
        acc[pl.ds(pl.multiple_of(b * WIDE + core * HALF, HALF), HALF), :] = own_ref[rows].astype(f32)
        acc[pl.ds(pl.multiple_of(b * WIDE + HALF - core * HALF, HALF), HALF), :] = other_ref[
            rows
        ].astype(f32)
    if group:
        total = acc[...]
        for h in range(group):
            skip = (group - h) * WIDE
            total = total - nt(earlier[h][skip:, :], earlier[h][skip : skip + WIDE, :])
        acc[...] = total
        whole[:first, :] = jnp.zeros((first, WIDE), f32)
    for start in range(0, WIDE, HALF):
        cols = slice(start, start + HALF)
        upper, inverse = eliminate(acc[cols, cols])
        inverse = inverse.astype(bf16)
        lower = upper.T
        whole[first + start : first + start + HALF, cols] = lower
        half_ref[cols, cols] = lower.astype(bf16)
        inverse_ref[cols, cols] = inverse
        if start:
            whole[first : first + start, cols] = jnp.zeros((start, HALF), f32)
            half_ref[:start, cols] = jnp.zeros((start, HALF), bf16)
            inverse_ref[:start, cols] = jnp.zeros((start, HALF), bf16)
            between = nn(half_ref[cols, :start], inverse_ref[:start, :start]).astype(bf16)
            inverse_ref[cols, :start] = (-nn(inverse, between)).astype(bf16)
        below = start + HALF
        if below < count:
            under = nt(acc[below:, cols].astype(bf16), inverse)
            whole[first + below :, cols] = under
            under = under.astype(bf16)
            half_ref[below:, cols] = under
            if below < WIDE:
                acc[below:, below:] = acc[below:, below:] - nt(under, under[: WIDE - below])
    slab = slab_ref.shape[0]
    slab_ref[...] = whole[pl.ds(pl.multiple_of(z * slab, slab), slab), :]


def mixed_body(parts, place, mask_ref, *refs):
    rights, panel_ref = refs[:parts], refs[parts]
    own_ref, away_ref, right = refs[parts + 1 :]
    slab = rights[0].shape[1]
    core, z = place[0], place[1]
    for d in range(parts):
        source = lax.rem(z - d + parts, parts)
        right[:, pl.ds(pl.multiple_of(source * slab, HALF), slab)] = rights[d][...]
    count, half = panel_ref.shape[1], panel_ref.shape[3] // 2
    for out, row in ((own_ref, core), (away_ref, 1 - core)):
        for j in range(count):
            rows = slice(j * half, (j + 1) * half)
            both = nn(right[rows, :], panel_ref[row, j])
            sign = -mask_ref[row, j].astype(f32)
            inner = (both[:, half:] * sign).astype(bf16)
            out[rows, :] = nt(inner, panel_ref[row, j, :, :half]).astype(bf16)


def apply_stage(value, inners, outers):
    total = None
    for inner, outer in zip(inners, outers):
        part = nn(nt(value, inner).astype(bf16), outer)
        total = part if total is None else total + part
    return total.astype(bf16)


def put_halves(value, refs):
    rows = value.shape[0] // 2
    refs[0][...] = value[:rows]
    refs[1][...] = value[rows:]


def get_halves(refs):
    low = refs[4][...]
    return low + jnp.concatenate(
        [refs[i][...].astype(f32) + refs[i + 2][...].astype(f32) for i in range(2)], axis=0
    )


def low_body(forward, place, value_ref, low_ref, out_ref):
    half = low_ref.shape[0] // 2
    up, down = low_ref[:half], low_ref[half:]
    inner, outer = (down, up) if forward else (up, down)
    out_ref[...] = nn(nt(value_ref[...], inner).astype(bf16), outer)


def first_body(place, value_ref, u0, u1, m0, m1, *outs):
    put_halves(apply_stage(value_ref[...], (u0[...], u1[...]), (m0[...], m1[...])), outs)


def middle_body(forward, place, a0, a1, b0, b1, low, u0, u1, m0, m1, value_ref, *outs):
    ups, downs = (m0[...], m1[...]), (u0[...], u1[...])
    value = get_halves((a0, a1, b0, b1, low)).astype(bf16)
    value_ref[...] = value
    inners, outers = (downs, ups) if forward else (ups, downs)
    put_halves(apply_stage(value, inners, outers), outs)


def basis_body(place, a0, a1, b0, b1, low, u0, u1, m0, m1, basis_ref, *outs):
    third = get_halves((a0, a1, b0, b1, low))
    gram = nt(third, third, precision=lax.Precision.HIGHEST)
    _, inverse = eliminate(gram)
    basis = nn(inverse, third, precision=lax.Precision.HIGHEST).astype(bf16)
    basis_ref[...] = basis
    put_halves(apply_stage(basis, (m0[...], m1[...]), (u0[...], u1[...])), outs)


def solve_body(groups, place, a0, a1, b0, b1, low, *refs):
    factors, inverses, out_ref = refs[:groups], refs[groups : 2 * groups], refs[2 * groups]
    value = get_halves((a0, a1, b0, b1, low))
    solved = []
    for g in range(groups):
        cols = slice(g * WIDE, (g + 1) * WIDE)
        rest = value[:, cols]
        for h in range(g):
            skip = (g - h) * WIDE
            rest = rest - nt(solved[h], factors[h][skip : skip + WIDE, :])
        solved.append(nt(rest.astype(bf16), inverses[g][...]).astype(bf16))
        out_ref[:, cols] = solved[g]


def finish_body(place, basis_own, basis_other, solved_own, solved_other, out_ref):
    core = place[0]
    half = basis_own.shape[0]
    for row, basis, solved in (
        (core, basis_own, solved_own),
        (1 - core, basis_other, solved_other),
    ):
        both = jnp.concatenate([basis[...], solved[...]], axis=0).astype(f32)
        out_ref[row] = both.T


def shards(panel, row_k, mask, a_low, a_diag, sketch):
    cols, parts = lax.axis_size("cols"), lax.axis_size("rows")
    here, z = lax.axis_index("cols"), lax.axis_index("rows")
    count, slab, width = row_k.shape
    half = width // 2
    order, rank = sketch.shape
    groups = order // WIDE
    piece = max(order // cols, 1)
    place = jnp.stack(
        [
            here % 2,
            z,
            here,
            here // 2,
            here * 0,
            here * piece // HALF,
            here * piece % HALF,
            here * piece % HALF + piece,
        ]
    ).astype(jnp.int32)
    partner = [(i, i ^ 1) for i in range(cols)]
    masks = [2 << i for i in range((cols // 2).bit_length() - 1)]

    def swap(value):
        return lax.ppermute(value, "cols", partner)

    def cross(value, bit):
        return lax.ppermute(value, "cols", [(i, i ^ bit) for i in range(cols)])

    def spread_rows(value):
        return [value] + [
            lax.ppermute(value, "rows", [(i, (i + d) % parts) for i in range(parts)])
            for d in range(1, parts)
        ]

    def add(first, second):
        return (first.astype(f32) + second.astype(f32)).astype(bf16)

    def sum_chips(pair):
        orders = (masks, masks[::-1])
        value = list(pair)
        for step in range(len(masks)):
            got = [cross(value[i], orders[i][step]) for i in range(2)]
            if step == len(masks) - 1:
                return value[0], value[1], got[0], got[1]
            value = [add(value[i], got[i]) for i in range(2)]

    blocks = -(-count // max(slab // half, 1))
    left, right, corner, low_t, sketch_t = call(
        prepare_body,
        "prepare",
        (
            shaped(((count + blocks) * half, slab), bf16),
            shaped((count * half, slab), bf16),
            shaped((slab, HALF), bf16),
            shaped((width, order), bf16),
            shaped((rank, order), bf16),
        ),
        place,
        row_k,
        a_diag,
        a_low,
        sketch,
    )
    lefts = spread_rows(left)
    corners = spread_rows(corner)
    rights = spread_rows(right)
    rest_rows = sum((groups - g) * HALF for g in range(1, groups))
    left_t, own0, own1, away0, away1 = call(
        functools.partial(diagonal_body, count, parts),
        "diagonal",
        (
            shaped((count * half, order), bf16),
            shaped((groups * HALF, WIDE), bf16),
            shaped((rest_rows, WIDE), bf16),
            shaped((groups * HALF, WIDE), bf16),
            shaped((rest_rows, WIDE), bf16),
        ),
        place,
        *lefts,
        *corners,
        scratch=(pltpu.VMEM((order, order), f32), pltpu.VMEM((count * half, order), bf16)),
    )

    def whole_chunk(own, away):
        value = add(own, swap(away))
        rows = value.shape[0] // 2
        a0, a1, b0, b1 = sum_chips((value[:rows], value[rows:]))
        value = jnp.concatenate([add(a0, b0), add(a1, b1)], axis=0)
        return value, swap(value)

    head = whole_chunk(own0, away0)
    tail = whole_chunk(own1, away1)
    left_other = swap(left_t)
    mixed_own, mixed_away = pl.pallas_call(
        functools.partial(mixed_body, parts),
        out_shape=(shaped((count * half, order), bf16),) * 2,
        in_specs=[SMEM, SMEM] + [VMEM] * (parts + 1),
        out_specs=(VMEM, VMEM),
        scratch_shapes=[pltpu.VMEM((count * half, order), bf16)],
        name="mixed",
    )(place, mask, *rights, panel)
    mixed_other = swap(mixed_away)
    factors = (left_t, left_other, mixed_own, mixed_other)
    pair = (shaped((rank // 2, order), bf16),) * 2

    slabs, halves, inverses = [], [], []
    at = 0
    for g in range(groups):
        rows = order - g * WIDE
        own, other = head if g == 0 else tail
        slab_part, half_part, inverse = call(
            functools.partial(factor_body, g, at),
            "factor%d" % g,
            (
                shaped((slab, WIDE), f32),
                shaped((rows, WIDE), bf16),
                shaped((WIDE, WIDE), bf16),
            ),
            place,
            own,
            other,
            *halves,
            scratch=(pltpu.VMEM((rows, WIDE), f32), pltpu.VMEM((order, WIDE), f32)),
        )
        if g:
            at += rows // 2
        slabs.append(slab_part)
        halves.append(half_part)
        inverses.append(inverse)
    diag_out = jnp.concatenate(slabs, axis=1)

    whole = shaped((rank, order), bf16)

    def low_term(value, forward):
        return call(
            functools.partial(low_body, forward),
            "low",
            shaped((rank, order), f32),
            place,
            value,
            low_t,
        )

    low = low_term(sketch_t, True)
    value = sum_chips(call(first_body, "first", pair, place, sketch_t, *factors))
    for forward, name in ((False, "second"), (True, "third")):
        start, *value = call(
            functools.partial(middle_body, forward),
            name,
            (whole,) + pair,
            place,
            *value,
            low,
            *factors,
        )
        low = low_term(start, forward)
        value = sum_chips(value)
    basis, *value = call(basis_body, "basis", (whole,) + pair, place, *value, low, *factors)
    low = low_term(basis, False)
    basis_other = swap(basis)
    value = sum_chips(value)
    solved = call(
        functools.partial(solve_body, groups),
        "solve",
        whole,
        place,
        *value,
        low,
        *halves,
        *inverses,
    )
    panel_out = call(
        finish_body,
        "finish",
        shaped((2, order, 2 * rank), f32),
        place,
        basis,
        basis_other,
        solved,
        swap(solved),
    )
    return panel_out, diag_out


def solution(mesh):
    return jax.shard_map(
        shards,
        mesh=mesh,
        in_specs=(
            P("rows", "cols", None, None),
            P("cols", "rows", None),
            P("rows", "cols"),
            P("rows", None, None),
            P("rows", None),
            P(),
        ),
        out_specs=(P("rows", None, None), P("rows", None)),
        check_vma=False,
    )
```

```python
import functools

import jax
import jax.numpy as jnp
from jax import lax
from jax.experimental import pallas as pl
from jax.experimental.pallas import tpu as pltpu
from jax.sharding import PartitionSpec as P


f32 = jnp.float32
bf16 = jnp.bfloat16
WIDE = 256
HALF = 128
ROOM = 4 << 20
SMEM = pl.BlockSpec(memory_space=pltpu.SMEM)
VMEM = pl.BlockSpec(memory_space=pltpu.VMEM)


def nt(first, second, **kw):
    return lax.dot_general(
        first, second, (((1,), (1,)), ((), ())), preferred_element_type=f32, **kw
    )


def tn(first, second):
    return lax.dot_general(first, second, (((0,), (0,)), ((), ())), preferred_element_type=f32)


def nn(first, second, **kw):
    return jnp.dot(first, second, preferred_element_type=f32, **kw)


def shaped(shape, kind):
    return jax.ShapeDtypeStruct(shape, kind)


def held(shape, kind):
    size = jnp.dtype(kind).itemsize
    for length in shape:
        size *= length
    return size


def call(body, outs, *args, scratch=(), scalars=1):
    room = sum(held(v.shape, v.dtype) for v in [*args, *jax.tree.leaves(outs), *scratch])
    return pl.pallas_call(
        body,
        out_shape=outs,
        in_specs=[SMEM] * scalars + [VMEM] * (len(args) - scalars),
        out_specs=jax.tree.map(lambda _: VMEM, outs),
        scratch_shapes=[pltpu.VMEM(v.shape, v.dtype) for v in scratch],
        compiler_params=pltpu.CompilerParams(vmem_limit_bytes=room + ROOM),
    )(*args)


def eliminate(block, zero):
    size = block.shape[0]
    lane = lax.broadcasted_iota(jnp.int32, (8, size), 1)
    sub = lax.broadcasted_iota(jnp.int32, (8, size), 0)
    tiles = [block[8 * g : 8 * g + 8] for g in range(size // 8)]

    def spread(tile, j):
        return jnp.broadcast_to(tile[:, j : j + 1], (8, size))

    def lift(tile, i):
        return jnp.broadcast_to(tile[i : i + 1], (8, size))

    uppers, inverses = [], []
    for own in range(size // 8):
        base = 8 * own
        inside = (lane >= base) & (lane < base + 8)
        plain = tiles[own]
        cols = [spread(plain, base + j) + zero for j in range(8)]
        full = jnp.where(inside, jnp.where(lane == base + sub, 1.0, 0.0), plain)
        rows, up, diag, blocks = full, full, full, []
        for k in range(0, 8, 2):
            one, two = cols[k], cols[k + 1]
            a, b, c = lift(one, k), lift(one, k + 1), lift(two, k + 1)
            over = 1.0 / (a * c - b * b)
            ratio = b * (1.0 / a)
            pivots = (sub == k) | (sub == k + 1)
            first = jnp.where(pivots, 0.0, one * c - two * b)
            second = jnp.where(pivots, 0.0, two * a - one * b)

            def cleared(value):
                return value - over * (first * lift(value, k) + second * lift(value, k + 1))

            def kept(into, value):
                into = jnp.where(sub == k + 1, value - ratio * lift(value, k), into)
                return jnp.where(sub == k, value, into)

            rows, up = kept(rows, full), kept(up, plain)
            diag = jnp.where(sub == k, a, jnp.where(sub == k + 1, c - b * ratio, diag))
            for j in range(k + 2, 8):
                cols[j] = cleared(cols[j])
            full = cleared(full)
            if k < 6:
                plain = cleared(plain)
            blocks.append((a * over, b * over, c * over))
        weights = []
        for k in range(0, 8, 2):
            a, b, c = blocks[k // 2]
            one, two = lift(full, k), lift(full, k + 1)
            weights += [c * one - b * two, a * two - b * one]
        for g in range(own + 1, size // 8):
            rest = jnp.where(inside, 0.0, tiles[g])
            even = spread(tiles[g], base) * weights[0]
            odd = spread(tiles[g], base + 1) * weights[1]
            for j in range(2, 8, 2):
                even = even + spread(tiles[g], base + j) * weights[j]
                odd = odd + spread(tiles[g], base + j + 1) * weights[j + 1]
            tiles[g] = rest - (even + odd)
        root = lax.rsqrt(diag)
        inverses.append(jnp.where(lane <= sub + base, rows * root, 0.0))
        uppers.append(jnp.where(lane >= sub + base, up * root, 0.0))
    return jnp.concatenate(uppers, 0), jnp.concatenate(inverses, 0)


def put_corner(corner_ref, start, stop, out_ref, at):
    rows, slab = corner_ref.shape[0], out_ref.shape[1]
    for k in range(start // slab, stop // slab):
        out_ref[at : at + rows, :] = corner_ref[:, k * slab : (k + 1) * slab]
        at += rows


def left_body(place, row_ref, corner_ref, left_ref):
    count, slab, width = row_ref.shape
    half = width // 2
    per = max(slab // half, 1)
    for j in range(count):
        left_ref[j * half : (j + 1) * half, :] = row_ref[j].T[:half]
        right = row_ref[j, :, half:]
        top, at = count * half + (j // per) * half, (j % per) * half
        if j % per == 0:
            left_ref[top : top + half, :] = jnp.zeros((half, slab), bf16)
        left_ref[top : top + half, at : at + half] = tn(right, right).astype(bf16)
    put_corner(corner_ref, 0, WIDE, left_ref, (count + -(-count // per)) * half)


def right_body(place, row_ref, low_ref, corner_ref, right_ref, low_t_ref):
    count, _, width = row_ref.shape
    half = width // 2
    for j in range(count):
        right_ref[j * half : (j + 1) * half, :] = row_ref[j].T[half:]
    put_corner(corner_ref, WIDE, corner_ref.shape[1], right_ref, count * half)
    low_t_ref[...] = low_ref[place[0]].T


def diagonal_body(count, parts, place, *refs):
    lefts = refs[:parts]
    left_ref, own0_ref, own1_ref, away0_ref, away1_ref, total, turned = refs[parts:]
    slab = lefts[0].shape[1]
    half = turned.shape[0] // count
    per = max(slab // half, 1)
    core, z = place[0], place[1]
    for d in range(parts):
        source = lax.rem(z - d + parts, parts)
        left_ref[:, pl.ds(pl.multiple_of(source * slab, HALF), slab)] = lefts[d][: count * half]
    for j in range(count):
        rows = slice(j * half, (j + 1) * half)
        top, at = count * half + (j // per) * half, (j % per) * half
        core_sum = sum(lefts[d][top : top + half, at : at + half].astype(f32) for d in range(parts))
        turned[rows, :] = (-nn(core_sum.astype(bf16), left_ref[rows, :])).astype(bf16)
    total[...] = tn(turned[...], left_ref[...])
    order = total.shape[0]
    for out0, out1, side in ((own0_ref, own1_ref, core), (away0_ref, away1_ref, 1 - core)):
        fill = 0
        for g in range(order // WIDE):
            for b in range(g, order // WIDE):
                from_row = pl.multiple_of(b * WIDE + side * HALF, HALF)
                value = total[pl.ds(from_row, HALF), g * WIDE : (g + 1) * WIDE].astype(bf16)
                if g == 0:
                    out0[b * HALF : (b + 1) * HALF, :] = value
                else:
                    out1[fill : fill + HALF, :] = value
                    fill += HALF


def join_body(at, start, stop, place, own_ref, got_ref, *refs):
    shards, out_ref, acc = refs[:-2], refs[-2], refs[-1]
    z, chip, parts = place[1], place[2], len(shards)
    acc[...] = own_ref[...].astype(f32) + got_ref[...].astype(f32)
    slab = shards[0].shape[1]
    per, blocks = WIDE // slab, parts * slab // WIDE
    rows = (shards[0].shape[0] - at) // (per * (stop - start))
    for d in range(parts):
        block = lax.rem(z - d + parts, parts) // per
        base = 0
        for g in range(start, stop):

            @pl.when(block >= g)
            def _(base=base, g=g):
                into = pl.ds(pl.multiple_of(base + (block - g) * HALF + chip * rows, 8), rows)
                for k in range(per):
                    lanes = slice(k * slab, (k + 1) * slab)
                    top = at + ((g - start) * per + k) * rows
                    acc[into, lanes] = acc[into, lanes] + shards[d][top : top + rows, :].astype(f32)

            base += (blocks - g) * HALF
    out_ref[...] = acc[...].astype(bf16)


def factor_body(group, at, place, own_ref, other_ref, *refs):
    earlier = refs[:group]
    slab_ref, half_ref, inverse_ref, whole = refs[group:]
    core, z = place[0], place[1]
    order = whole.shape[0]
    first, wide = group * HALF, group * HALF // WIDE
    lanes = slice(first - wide * WIDE, first - wide * WIDE + HALF)
    blocks = []
    for r in range(group, order // HALF):
        rows = slice(at + (r // 2 - wide) * HALF, at + (r // 2 - wide + 1) * HALF)
        mine = own_ref[rows, lanes].astype(f32)
        blocks.append(jnp.where(core == r % 2, mine, other_ref[rows, lanes].astype(f32)))
    total = jnp.concatenate(blocks, axis=0)
    for h in range(group):
        skip = (group - h) * HALF
        total = total - nt(earlier[h][skip:, :], earlier[h][skip : skip + HALF, :])
    upper, inverse = eliminate(total[:HALF], place[4].astype(f32))
    inverse = inverse.astype(bf16)
    lower = upper.T
    if group:
        whole[:first, :] = jnp.zeros((first, HALF), f32)
    whole[first : first + HALF, :] = lower
    half_ref[:HALF, :] = lower.astype(bf16)
    inverse_ref[...] = inverse
    if first + HALF < order:
        under = nt(total[HALF:].astype(bf16), inverse)
        whole[first + HALF :, :] = under
        half_ref[HALF:, :] = under.astype(bf16)
    slab = slab_ref.shape[0]
    slab_ref[...] = whole[pl.ds(pl.multiple_of(z * slab, slab), slab), :]


def mixed_body(parts, place, mask_ref, *refs):
    rights, panel_ref = refs[:parts], refs[parts]
    own_ref, away_ref, right = refs[parts + 1 :]
    slab = rights[0].shape[1]
    core, z = place[0], place[1]
    for d in range(parts):
        source = lax.rem(z - d + parts, parts)
        right[:, pl.ds(pl.multiple_of(source * slab, HALF), slab)] = rights[d][: right.shape[0]]
    count, half = panel_ref.shape[1], panel_ref.shape[3] // 2
    for out, row in ((own_ref, core), (away_ref, 1 - core)):
        for j in range(count):
            rows = slice(j * half, (j + 1) * half)
            both = nn(right[rows, :], panel_ref[row, j])
            sign = -mask_ref[row, j].astype(f32)
            inner = (both[:, half:] * sign).astype(bf16)
            out[rows, :] = nt(inner, panel_ref[row, j, :, :half]).astype(bf16)


def apply_stage(value, inners, outers):
    total = None
    for inner, outer in zip(inners, outers):
        part = nn(nt(value, inner).astype(bf16), outer)
        total = part if total is None else total + part
    return total.astype(bf16)


def low_body(forward, place, value_ref, low_ref, out_ref):
    half = low_ref.shape[0] // 2
    up, down = low_ref[:half], low_ref[half:]
    inner, outer = (down, up) if forward else (up, down)
    out_ref[...] = nn(nt(value_ref[...], inner).astype(bf16), outer)


def first_body(place, value_ref, u0, u1, m0, m1, out_ref):
    out_ref[...] = apply_stage(value_ref[...], (u0[...], u1[...]), (m0[...], m1[...]))


def joined(own, got, low):
    return low[...] + (own[...].astype(f32) + got[...].astype(f32))


def middle_body(forward, place, own, got, low, u0, u1, m0, m1, value_ref, out_ref):
    ups, downs = (m0[...], m1[...]), (u0[...], u1[...])
    value = joined(own, got, low).astype(bf16)
    value_ref[...] = value
    inners, outers = (downs, ups) if forward else (ups, downs)
    out_ref[...] = apply_stage(value, inners, outers)


def basis_body(place, own, got, low, u0, u1, m0, m1, basis_ref, out_ref):
    third = joined(own, got, low)
    gram = nt(third, third, precision=lax.Precision.HIGHEST)
    _, inverse = eliminate(gram, place[4].astype(f32))
    basis = nn(inverse, third, precision=lax.Precision.HIGHEST).astype(bf16)
    basis_ref[...] = basis
    out_ref[...] = apply_stage(basis, (m0[...], m1[...]), (u0[...], u1[...]))


def solve_body(groups, place, basis, own, got, low, *refs):
    factors, inverses, out_ref = refs[:groups], refs[groups : 2 * groups], refs[2 * groups]
    rest = joined(own, got, low)
    rank = rest.shape[0]
    out_ref[:rank] = basis[...]
    for g in range(groups):
        solved = nt(rest[:, :HALF].astype(bf16), inverses[g][...]).astype(bf16)
        out_ref[rank:, g * HALF : (g + 1) * HALF] = solved
        if g < groups - 1:
            rest = rest[:, HALF:] - nt(solved, factors[g][HALF:, :])


def finish_body(place, own, other, out_ref):
    out_ref[place[0]] = own[...].astype(f32).T
    out_ref[1 - place[0]] = other[...].astype(f32).T


def after(value, *others):
    return lax.optimization_barrier((value, *others))[0]


def panel_step(panel, row_k, mask, a_low, a_diag, sketch):
    cols, parts = lax.axis_size("cols"), lax.axis_size("rows")
    here, z = lax.axis_index("cols"), lax.axis_index("rows")
    core, chip, chips = here % 2, here // 2, cols // 2
    count, slab, width = row_k.shape
    half = width // 2
    order, rank = sketch.shape
    groups = order // HALF
    partner = [(i, i ^ 1) for i in range(cols)]
    masks = [2 << i for i in range((cols // 2).bit_length() - 1)]
    place = jnp.stack([core, z, chip, here, here * 0]).astype(jnp.int32)

    def swap(value):
        return lax.ppermute(value, "cols", partner)

    def cross(value, step):
        bits = masks[step], masks[len(masks) - 1 - step]
        return lax.ppermute(value, "cols", [(i, i ^ bits[i % 2]) for i in range(cols)])

    def spread_rows(value):
        return [value] + [
            lax.ppermute(value, "rows", [(i, (i + d) % parts) for i in range(parts)])
            for d in range(1, parts)
        ]

    def add(*values):
        return sum(value.astype(f32) for value in values).astype(bf16)

    def sum_chips(value, fill=lambda value: ()):
        for step in range(len(masks)):
            got = cross(value, step)
            got = after(got, *fill(value))
            if step == len(masks) - 1:
                return value, got
            value = add(value, got)

    own_rows = a_diag[:HALF] if slab == HALF else lax.dynamic_slice_in_dim(a_diag, core * HALF, HALF, 0)
    corner = lax.dynamic_slice_in_dim(own_rows, chip * (HALF // chips), HALF // chips, 0)
    if slab == HALF:
        corner = jnp.where(z % 2 == core, corner, 0.0)
    corner = corner.astype(bf16)
    left_rows = (count + -(-count // max(slab // half, 1))) * half
    left = call(
        left_body,
        shaped((left_rows + WIDE // slab * (HALF // chips), slab), bf16),
        place,
        row_k,
        corner,
    )
    lefts = spread_rows(left)
    right, low_t = call(
        right_body,
        (
            shaped((count * half + (order - WIDE) // slab * (HALF // chips), slab), bf16),
            shaped((width, order), bf16),
        ),
        place,
        row_k,
        a_low,
        corner,
    )
    sketch_t = sketch.T
    rights = spread_rows(after(right, *lefts))
    rest_rows = sum(order // 2 - g * HALF for g in range(1, order // WIDE))
    left_t, own0, own1, away0, away1 = call(
        functools.partial(diagonal_body, count, parts),
        (
            shaped((count * half, order), bf16),
            shaped((order // 2, WIDE), bf16),
            shaped((rest_rows, WIDE), bf16),
            shaped((order // 2, WIDE), bf16),
            shaped((rest_rows, WIDE), bf16),
        ),
        place,
        after(lefts[0], right),
        *lefts[1:],
        scratch=(shaped((order, order), f32), shaped((count * half, order), bf16)),
    )

    def chunk_half(own, away, shards, at, start, stop, fill=lambda value: ()):
        got = swap(away)
        value = call(
            functools.partial(join_body, at, start, stop),
            shaped(own.shape, bf16),
            place,
            own,
            got,
            *shards,
            scratch=(shaped(own.shape, f32),),
        )
        return add(*sum_chips(value, fill))

    head_half = chunk_half(own0, away0, lefts, left_rows, 0, 1)
    head = head_half, swap(head_half)
    left_other = swap(left_t)
    chunks, mixed = [head], []
    slabs, halves, inverses = [], [], []

    def factor(*earlier):
        g = len(halves)
        if g >= groups:
            return ()
        wide = g * HALF // WIDE
        own, other = chunks[min(wide, 1)]
        done = sum(order // 2 - w * HALF for w in range(1, wide))
        slab_part, half_part, inverse = call(
            functools.partial(factor_body, g, done),
            (
                shaped((slab, HALF), f32),
                shaped((order - g * HALF, HALF), bf16),
                shaped((HALF, HALF), bf16),
            ),
            place,
            after(own, *earlier),
            other,
            *halves,
            scratch=(shaped((order, HALF), f32),),
        )
        slabs.append(slab_part)
        halves.append(half_part)
        inverses.append(inverse)
        return (inverse,)

    def mix(*earlier):
        if not mixed:
            mixed.extend(
                call(
                    functools.partial(mixed_body, parts),
                    (shaped((count * half, order), bf16),) * 2,
                    place,
                    mask,
                    after(rights[0], *earlier),
                    *rights[1:],
                    panel,
                    scratch=(shaped((count * half, order), bf16),),
                    scalars=2,
                )
            )
        return tuple(mixed)

    def tail_fill(value):
        return mix(value) if halves else factor(value)

    tail_half = chunk_half(
        own1, after(away1, head_half), rights, count * half, 1, order // WIDE, tail_fill
    )
    chunks.append((tail_half, swap(tail_half)))
    mixed_own, mixed_away = mix()
    mixed_other = swap(mixed_away)
    factors = (left_t, left_other, mixed_own, mixed_other)
    whole = shaped((rank, order), bf16)

    def low_term(value, forward):
        return call(
            functools.partial(low_body, forward), shaped((rank, order), f32), place, value, low_t
        )

    def fill(value):
        return factor(value)

    low = low_term(sketch_t, True)
    done = factor(mixed_away)
    value = call(first_body, whole, place, after(sketch_t, *done, tail_half), *factors)
    value = sum_chips(value, fill)
    for forward in (False, True):
        start, value = call(
            functools.partial(middle_body, forward), (whole, whole), place, *value, low, *factors
        )
        low = low_term(start, forward)
        value = sum_chips(value, fill)
    basis, value = call(basis_body, (whole, whole), place, *value, low, *factors)
    low = low_term(basis, False)
    value = sum_chips(value, fill)
    while len(halves) < groups:
        factor()
    diag_out = jnp.concatenate(slabs, axis=1)
    both = call(
        functools.partial(solve_body, groups),
        shaped((2 * rank, order), bf16),
        place,
        basis,
        *value,
        low,
        *halves,
        *inverses,
    )
    panel_out = call(finish_body, shaped((2, order, 2 * rank), f32), place, both, swap(both))
    return panel_out, diag_out


def solution(mesh):
    return jax.shard_map(
        panel_step,
        mesh=mesh,
        in_specs=(
            P("rows", "cols", None, None),
            P("cols", "rows", None),
            P("rows", "cols"),
            P("rows", None, None),
            P("rows", None),
            P(),
        ),
        out_specs=(P("rows", None, None), P("rows", None)),
        check_vma=False,
    )
```

```python
import functools

import jax
import jax.numpy as jnp
from jax import lax
from jax.experimental import pallas as pl
from jax.experimental.pallas import tpu as pltpu
from jax.sharding import PartitionSpec as P


f32 = jnp.float32
bf16 = jnp.bfloat16
WIDE = 256
HALF = 128
ROOM = 4 << 20
SMEM = pl.BlockSpec(memory_space=pltpu.SMEM)
VMEM = pl.BlockSpec(memory_space=pltpu.VMEM)


def nt(first, second, **kw):
    return lax.dot_general(
        first, second, (((1,), (1,)), ((), ())), preferred_element_type=f32, **kw
    )


def tn(first, second):
    return lax.dot_general(first, second, (((0,), (0,)), ((), ())), preferred_element_type=f32)


def nn(first, second, **kw):
    return jnp.dot(first, second, preferred_element_type=f32, **kw)


def shaped(shape, kind):
    return jax.ShapeDtypeStruct(shape, kind)


def held(shape, kind):
    size = jnp.dtype(kind).itemsize
    for length in shape:
        size *= length
    return size


def call(body, outs, *args, scratch=(), scalars=1):
    room = sum(held(v.shape, v.dtype) for v in [*args, *jax.tree.leaves(outs), *scratch])
    return pl.pallas_call(
        body,
        out_shape=outs,
        in_specs=[SMEM] * scalars + [VMEM] * (len(args) - scalars),
        out_specs=jax.tree.map(lambda _: VMEM, outs),
        scratch_shapes=[pltpu.VMEM(v.shape, v.dtype) for v in scratch],
        compiler_params=pltpu.CompilerParams(vmem_limit_bytes=room + ROOM),
    )(*args)


def eliminate(block, zero):
    size = block.shape[0]
    lane = lax.broadcasted_iota(jnp.int32, (8, size), 1)
    sub = lax.broadcasted_iota(jnp.int32, (8, size), 0)
    tiles = [block[8 * g : 8 * g + 8] for g in range(size // 8)]

    def spread(tile, j):
        return jnp.broadcast_to(tile[:, j : j + 1], (8, size))

    def lift(tile, i):
        return jnp.broadcast_to(tile[i : i + 1], (8, size))

    uppers, inverses = [], []
    for own in range(size // 8):
        base = 8 * own
        inside = (lane >= base) & (lane < base + 8)
        plain = tiles[own]
        cols = [spread(plain, base + j) + zero for j in range(8)]
        full = jnp.where(inside, jnp.where(lane == base + sub, 1.0, 0.0), plain)
        rows, up, diag, blocks = full, full, full, []
        for k in range(0, 8, 2):
            one, two = cols[k], cols[k + 1]
            a, b, c = lift(one, k), lift(one, k + 1), lift(two, k + 1)
            over = 1.0 / (a * c - b * b)
            ratio = b * (1.0 / a)
            pivots = (sub == k) | (sub == k + 1)
            first = jnp.where(pivots, 0.0, one * c - two * b)
            second = jnp.where(pivots, 0.0, two * a - one * b)

            def cleared(value):
                return value - over * (first * lift(value, k) + second * lift(value, k + 1))

            def kept(into, value):
                into = jnp.where(sub == k + 1, value - ratio * lift(value, k), into)
                return jnp.where(sub == k, value, into)

            rows, up = kept(rows, full), kept(up, plain)
            diag = jnp.where(sub == k, a, jnp.where(sub == k + 1, c - b * ratio, diag))
            for j in range(k + 2, 8):
                cols[j] = cleared(cols[j])
            full = cleared(full)
            if k < 6:
                plain = cleared(plain)
            blocks.append((a * over, b * over, c * over))
        weights = []
        for k in range(0, 8, 2):
            a, b, c = blocks[k // 2]
            one, two = lift(full, k), lift(full, k + 1)
            weights += [c * one - b * two, a * two - b * one]
        for g in range(own + 1, size // 8):
            rest = jnp.where(inside, 0.0, tiles[g])
            even = spread(tiles[g], base) * weights[0]
            odd = spread(tiles[g], base + 1) * weights[1]
            for j in range(2, 8, 2):
                even = even + spread(tiles[g], base + j) * weights[j]
                odd = odd + spread(tiles[g], base + j + 1) * weights[j + 1]
            tiles[g] = rest - (even + odd)
        root = lax.rsqrt(diag)
        inverses.append(jnp.where(lane <= sub + base, rows * root, 0.0))
        uppers.append(jnp.where(lane >= sub + base, up * root, 0.0))
    return jnp.concatenate(uppers, 0), jnp.concatenate(inverses, 0)


def put_corner(corner_ref, start, stop, out_ref, at):
    rows, slab = corner_ref.shape[0], out_ref.shape[1]
    for k in range(start // slab, stop // slab):
        out_ref[at : at + rows, :] = corner_ref[:, k * slab : (k + 1) * slab]
        at += rows


def left_body(place, row_ref, corner_ref, left_ref):
    count, slab, width = row_ref.shape
    half = width // 2
    per = max(slab // half, 1)
    for j in range(count):
        left_ref[j * half : (j + 1) * half, :] = row_ref[j].T[:half]
        right = row_ref[j, :, half:]
        top, at = count * half + (j // per) * half, (j % per) * half
        if j % per == 0:
            left_ref[top : top + half, :] = jnp.zeros((half, slab), bf16)
        left_ref[top : top + half, at : at + half] = tn(right, right).astype(bf16)
    put_corner(corner_ref, 0, WIDE, left_ref, (count + -(-count // per)) * half)


def right_body(place, row_ref, low_ref, corner_ref, right_ref, low_t_ref):
    count, _, width = row_ref.shape
    half = width // 2
    for j in range(count):
        right_ref[j * half : (j + 1) * half, :] = row_ref[j].T[half:]
    put_corner(corner_ref, WIDE, corner_ref.shape[1], right_ref, count * half)
    low_t_ref[...] = low_ref[place[0]].T


def diagonal_body(count, parts, place, *refs):
    lefts = refs[:parts]
    left_ref, own0_ref, own1_ref, away0_ref, away1_ref, total, turned = refs[parts:]
    slab = lefts[0].shape[1]
    half = turned.shape[0] // count
    per = max(slab // half, 1)
    core, z = place[0], place[1]
    for d in range(parts):
        source = lax.rem(z - d + parts, parts)
        left_ref[:, pl.ds(pl.multiple_of(source * slab, HALF), slab)] = lefts[d][: count * half]
    for j in range(count):
        rows = slice(j * half, (j + 1) * half)
        top, at = count * half + (j // per) * half, (j % per) * half
        core_sum = sum(lefts[d][top : top + half, at : at + half].astype(f32) for d in range(parts))
        turned[rows, :] = (-nn(core_sum.astype(bf16), left_ref[rows, :])).astype(bf16)
    total[...] = tn(turned[...], left_ref[...])
    order = total.shape[0]
    for out0, out1, side in ((own0_ref, own1_ref, core), (away0_ref, away1_ref, 1 - core)):
        fill = 0
        for g in range(order // WIDE):
            for b in range(g, order // WIDE):
                from_row = pl.multiple_of(b * WIDE + side * HALF, HALF)
                value = total[pl.ds(from_row, HALF), g * WIDE : (g + 1) * WIDE].astype(bf16)
                if g == 0:
                    out0[b * HALF : (b + 1) * HALF, :] = value
                else:
                    out1[fill : fill + HALF, :] = value
                    fill += HALF


def join_body(at, parts, start, stop, place, own_ref, got_ref, *refs):
    shards, outs, acc = refs[:parts], refs[parts:-1], refs[-1]
    z, chip = place[1], place[2]
    acc[...] = own_ref[...].astype(f32) + got_ref[...].astype(f32)
    slab = shards[0].shape[1]
    per, blocks = WIDE // slab, parts * slab // WIDE
    rows = (shards[0].shape[0] - at) // (per * (stop - start))
    for d in range(parts):
        block = lax.rem(z - d + parts, parts) // per
        base = 0
        for g in range(start, stop):

            @pl.when(block >= g)
            def _(base=base, g=g):
                into = pl.ds(pl.multiple_of(base + (block - g) * HALF + chip * rows, 8), rows)
                for k in range(per):
                    lanes = slice(k * slab, (k + 1) * slab)
                    top = at + ((g - start) * per + k) * rows
                    acc[into, lanes] = acc[into, lanes] + shards[d][top : top + rows, :].astype(f32)

            base += (blocks - g) * HALF
    top = 0
    for out in outs:
        out[...] = acc[top : top + out.shape[0], :].astype(bf16)
        top += out.shape[0]


def factor_body(group, at, place, own_ref, other_ref, *refs):
    earlier = refs[:group]
    slab_ref, half_ref, inverse_ref, whole = refs[group:]
    core, z = place[0], place[1]
    order = whole.shape[0]
    first, wide = group * HALF, group * HALF // WIDE
    lanes = slice(first - wide * WIDE, first - wide * WIDE + HALF)
    blocks = []
    for r in range(group, order // HALF):
        rows = slice(at + (r // 2 - wide) * HALF, at + (r // 2 - wide + 1) * HALF)
        mine = own_ref[rows, lanes].astype(f32)
        blocks.append(jnp.where(core == r % 2, mine, other_ref[rows, lanes].astype(f32)))
    total = jnp.concatenate(blocks, axis=0)
    for h in range(group):
        skip = (group - h) * HALF
        total = total - nt(earlier[h][skip:, :], earlier[h][skip : skip + HALF, :])
    upper, inverse = eliminate(total[:HALF], place[4].astype(f32))
    inverse = inverse.astype(bf16)
    lower = upper.T
    if group:
        whole[:first, :] = jnp.zeros((first, HALF), f32)
    whole[first : first + HALF, :] = lower
    half_ref[:HALF, :] = lower.astype(bf16)
    inverse_ref[...] = inverse
    if first + HALF < order:
        under = nt(total[HALF:].astype(bf16), inverse)
        whole[first + HALF :, :] = under
        half_ref[HALF:, :] = under.astype(bf16)
    slab = slab_ref.shape[0]
    slab_ref[...] = whole[pl.ds(pl.multiple_of(z * slab, slab), slab), :]


def mixed_body(parts, place, mask_ref, *refs):
    rights, panel_ref = refs[:parts], refs[parts]
    own_ref, away_ref, right = refs[parts + 1 :]
    slab = rights[0].shape[1]
    core, z = place[0], place[1]
    for d in range(parts):
        source = lax.rem(z - d + parts, parts)
        right[:, pl.ds(pl.multiple_of(source * slab, HALF), slab)] = rights[d][: right.shape[0]]
    count, half = panel_ref.shape[1], panel_ref.shape[3] // 2
    for out, row in ((own_ref, core), (away_ref, 1 - core)):
        for j in range(count):
            rows = slice(j * half, (j + 1) * half)
            both = nn(right[rows, :], panel_ref[row, j])
            sign = -mask_ref[row, j].astype(f32)
            inner = (both[:, half:] * sign).astype(bf16)
            out[rows, :] = nt(inner, panel_ref[row, j, :, :half]).astype(bf16)


def apply_stage(value, inners, outers):
    total = None
    for inner, outer in zip(inners, outers):
        part = nn(nt(value, inner).astype(bf16), outer)
        total = part if total is None else total + part
    return total.astype(bf16)


def low_body(forward, place, value_ref, low_ref, out_ref):
    half = low_ref.shape[0] // 2
    up, down = low_ref[:half], low_ref[half:]
    inner, outer = (down, up) if forward else (up, down)
    out_ref[...] = nn(nt(value_ref[...], inner).astype(bf16), outer)


def first_body(place, value_ref, u0, u1, m0, m1, out_ref):
    out_ref[...] = apply_stage(value_ref[...], (u0[...], u1[...]), (m0[...], m1[...]))


def joined(own, got, low):
    return low[...] + (own[...].astype(f32) + got[...].astype(f32))


def middle_body(forward, place, own, got, low, u0, u1, m0, m1, value_ref, out_ref):
    ups, downs = (m0[...], m1[...]), (u0[...], u1[...])
    value = joined(own, got, low).astype(bf16)
    value_ref[...] = value
    inners, outers = (downs, ups) if forward else (ups, downs)
    out_ref[...] = apply_stage(value, inners, outers)


def basis_body(place, own, got, low, u0, u1, m0, m1, basis_ref, out_ref):
    third = joined(own, got, low)
    gram = nt(third, third, precision=lax.Precision.HIGHEST)
    _, inverse = eliminate(gram, place[4].astype(f32))
    basis = nn(inverse, third, precision=lax.Precision.HIGHEST).astype(bf16)
    basis_ref[...] = basis
    out_ref[...] = apply_stage(basis, (m0[...], m1[...]), (u0[...], u1[...]))


def solve_body(groups, place, basis, own, got, low, *refs):
    factors, inverses, out_ref = refs[:groups], refs[groups : 2 * groups], refs[2 * groups]
    rest = joined(own, got, low)
    rank = rest.shape[0]
    out_ref[:rank] = basis[...]
    for g in range(groups):
        solved = nt(rest[:, :HALF].astype(bf16), inverses[g][...]).astype(bf16)
        out_ref[rank:, g * HALF : (g + 1) * HALF] = solved
        if g < groups - 1:
            rest = rest[:, HALF:] - nt(solved, factors[g][HALF:, :])


def finish_body(place, own, other, out_ref):
    out_ref[place[0]] = own[...].astype(f32).T
    out_ref[1 - place[0]] = other[...].astype(f32).T


def after(value, *others):
    return lax.optimization_barrier((value, *others))[0]


def panel_step(panel, row_k, mask, a_low, a_diag, sketch):
    cols, parts = lax.axis_size("cols"), lax.axis_size("rows")
    here, z = lax.axis_index("cols"), lax.axis_index("rows")
    core, chip, chips = here % 2, here // 2, cols // 2
    count, slab, width = row_k.shape
    half = width // 2
    order, rank = sketch.shape
    groups = order // HALF
    partner = [(i, i ^ 1) for i in range(cols)]
    masks = [2 << i for i in range((cols // 2).bit_length() - 1)]
    place = jnp.stack([core, z, chip, here, here * 0]).astype(jnp.int32)

    def swap(value):
        return lax.ppermute(value, "cols", partner)

    def cross(value, step):
        bits = masks[step], masks[len(masks) - 1 - step]
        return lax.ppermute(value, "cols", [(i, i ^ bits[i % 2]) for i in range(cols)])

    def spread_rows(value):
        return [value] + [
            lax.ppermute(value, "rows", [(i, (i + d) % parts) for i in range(parts)])
            for d in range(1, parts)
        ]

    def add(*values):
        return sum(value.astype(f32) for value in values).astype(bf16)

    own_rows = a_diag[:HALF] if slab == HALF else lax.dynamic_slice_in_dim(a_diag, core * HALF, HALF, 0)
    corner = lax.dynamic_slice_in_dim(own_rows, chip * (HALF // chips), HALF // chips, 0)
    if slab == HALF:
        corner = jnp.where(z % 2 == core, corner, 0.0)
    corner = corner.astype(bf16)
    left_rows = (count + -(-count // max(slab // half, 1))) * half
    left = call(
        left_body,
        shaped((left_rows + WIDE // slab * (HALF // chips), slab), bf16),
        place,
        row_k,
        corner,
    )
    lefts = spread_rows(left)
    right, low_t = call(
        right_body,
        (
            shaped((count * half + (order - WIDE) // slab * (HALF // chips), slab), bf16),
            shaped((width, order), bf16),
        ),
        place,
        row_k,
        a_low,
        corner,
    )
    sketch_t = sketch.T
    rights = spread_rows(after(right, *lefts))
    rest_rows = sum(order // 2 - g * HALF for g in range(1, order // WIDE))
    left_t, own0, own1, away0, away1 = call(
        functools.partial(diagonal_body, count, parts),
        (
            shaped((count * half, order), bf16),
            shaped((order // 2, WIDE), bf16),
            shaped((rest_rows, WIDE), bf16),
            shaped((order // 2, WIDE), bf16),
            shaped((rest_rows, WIDE), bf16),
        ),
        place,
        after(lefts[0], right),
        *lefts[1:],
        scratch=(shaped((order, order), f32), shaped((count * half, order), bf16)),
    )

    def join(own, away, shards, at, start, stop, outs):
        got = swap(away)
        return call(
            functools.partial(join_body, at, parts, start, stop),
            outs,
            place,
            own,
            got,
            *shards,
            scratch=(shaped(own.shape, f32),),
        )

    whole = shaped((rank, order), bf16)
    steps, chunks = len(masks), []
    slabs, halves, inverses = [], [], []

    def factor(*earlier):
        g = len(halves)
        if g >= groups:
            return ()
        index, done = place_of[g * HALF // WIDE]
        if index >= len(chunks):
            return ()
        own, other = chunks[index]
        slab_part, half_part, inverse = call(
            functools.partial(factor_body, g, done),
            (
                shaped((slab, HALF), f32),
                shaped((order - g * HALF, HALF), bf16),
                shaped((HALF, HALF), bf16),
            ),
            place,
            after(own, *earlier),
            other,
            *halves,
            scratch=(shaped((order, HALF), f32),),
        )
        slabs.append(slab_part)
        halves.append(half_part)
        inverses.append(inverse)
        return (inverse,)

    def low_term(value, forward):
        return call(
            functools.partial(low_body, forward), shaped((rank, order), f32), place, value, low_t
        )

    head = join(own0, away0, lefts, left_rows, 0, 1, shaped(own0.shape, bf16))
    low = low_term(after(sketch_t, right), True)
    left_other = swap(left_t)
    mixed_own, mixed_away = call(
        functools.partial(mixed_body, parts),
        (shaped((count * half, order), bf16),) * 2,
        place,
        mask,
        after(rights[0], head, low),
        *rights[1:],
        panel,
        scratch=(shaped((count * half, order), bf16),),
        scalars=2,
    )
    mixed_other = swap(mixed_away)
    factors = (left_t, left_other, mixed_own, mixed_other)
    for step in range(steps):
        got = cross(after(head, mixed_away) if step == 1 else head, step)
        head = add(head, got)
    chunks.append((head, swap(head)))

    wides = order // WIDE
    sizes = [order // 2 - g * HALF for g in range(wides)]
    split = next(g for g in range(2, wides + 1) if 2 * sum(sizes[1:g]) >= rest_rows)
    place_of = {0: (0, 0)}
    for g in range(1, wides):
        start = 1 if g < split else split
        place_of[g] = (1 if g < split else 2, sum(sizes[start:g]))
    value = call(first_body, whole, place, after(sketch_t, low), *factors)
    parts_of_tail = (
        shaped((sum(sizes[1:split]), WIDE), bf16),
        shaped((sum(sizes[split:]), WIDE), bf16),
    )
    tail = list(join(own1, away1, rights, count * half, 1, wides, parts_of_tail))
    queue = [(i, step) for i in range(2) for step in range(steps)]
    flying = {}

    def launch(*earlier):
        if queue:
            i, step = queue.pop(0)
            tail[i] = after(tail[i], *earlier)
            flying[i] = cross(tail[i], step), step

    def land(*earlier):
        if not flying:
            return ()
        i, (got, step) = flying.popitem()
        tail[i] = add(tail[i], after(got, *earlier))
        if step == steps - 1:
            chunks.append((tail[i], swap(tail[i])))
        return (tail[i],)

    def sum_chips(value):
        for step in range(steps):
            got = cross(value, step)
            if not flying:
                launch(value)
            done = factor(value)
            got = after(got, *done)
            landed = land(*done)
            launch(*landed)
            if step == steps - 1:
                return value, after(got, *landed)
            value = add(value, got)
            value = after(value, *landed)

    launch(value)
    value = sum_chips(value)
    for forward in (False, True):
        start, value = call(
            functools.partial(middle_body, forward), (whole, whole), place, *value, low, *factors
        )
        low = low_term(start, forward)
        value = sum_chips(value)
    basis, value = call(basis_body, (whole, whole), place, *value, low, *factors)
    low = low_term(basis, False)
    value = sum_chips(value)
    while queue or flying:
        land()
        launch()
    while len(halves) < groups:
        factor()
    diag_out = jnp.concatenate(slabs, axis=1)
    both = call(
        functools.partial(solve_body, groups),
        shaped((2 * rank, order), bf16),
        place,
        basis,
        *value,
        low,
        *halves,
        *inverses,
    )
    panel_out = call(finish_body, shaped((2, order, 2 * rank), f32), place, both, swap(both))
    return panel_out, diag_out


def solution(mesh):
    return jax.shard_map(
        panel_step,
        mesh=mesh,
        in_specs=(
            P("rows", "cols", None, None),
            P("cols", "rows", None),
            P("rows", "cols"),
            P("rows", None, None),
            P("rows", None),
            P(),
        ),
        out_specs=(P("rows", None, None), P("rows", None)),
        check_vma=False,
    )
```
